128 devices in a mesh: grp: 8 (over y, core), mem: 16 (over z, x).
Axes of the slice: x: 4, y: 4, z: 4, core: 2. Of those that a mesh axis runs over, the one named last changes fastest.
Arguments:
- vectors: bfloat16 [131072, 768], P(('grp', 'mem')), may hold values from -6 to 6
- parents: int32 [131072], P(('grp', 'mem')), may hold values from 0 to 1
- children: int32 [131072], P(('grp', 'mem')), may hold values from 0 to 1023
- counts: int32 [128, 8], P(('grp', 'mem')), may hold values from 54 to 256, as said below
Outputs:
- distances: float32 [262144, 1024], P(('grp', 'mem'))
The draws below stay inside these ranges and needn't reach their ends.
Inputs may be any that keep to these rules, and one draw needn't show every extreme that they name: Each row of counts sums to 1024; shard d's vectors go to group 0 first, then group 1, and so on, in that many rows each. In every draw some group receives 256 vectors from every storage shard.
All inputs are finite; a program needn't handle non-finite values.
Results may differ from the reference program's by a relative error of at most 0.00055.
Values may be sent and summed in bfloat16 or wider, within the bound.
No kernel may reach another device: no remote copies, remote signals or barrier semaphores. Data moves between devices by JAX's collectives and lax.ppermute only.
A program may use at most 128 MiB of HBM per device.

```python
import math
import jax
import jax.numpy as jnp
import numpy as np
from jax import lax

D = 768
CHILD = 1024
PAR_GRP = 2
VEC_DEV = 1024
GROUPS = 8
STORES = 128
SHARD_GROUP_SLOTS = 256
ROWS = 131072
N_GRP = 8
N_MEM = 16


def draw_counts(key, part):
    heavy_key, weight_key = jax.random.split(jax.random.fold_in(key, 11), 2)
    heavy_group = jax.random.randint(heavy_key, (), 0, GROUPS)
    weights = jax.random.randint(weight_key, (STORES, GROUPS), 1, 3)
    heavy_flag = jnp.arange(GROUPS)[None, :] == heavy_group
    weights = jnp.where(heavy_flag, 0, weights)
    remaining = VEC_DEV - SHARD_GROUP_SLOTS
    weight_total = jnp.sum(weights, axis=1, keepdims=True)
    even_row_share = remaining * weights // weight_total
    remainder_rows = remaining - jnp.sum(even_row_share, axis=1, keepdims=True)
    rank_positions = jnp.cumsum(jnp.where(heavy_flag, 0, 1), axis=1)
    extra_row_count = jnp.where(jnp.logical_and(jnp.logical_not(heavy_flag), rank_positions <= remainder_rows), 1, 0)
    return jnp.where(heavy_flag, SHARD_GROUP_SLOTS, even_row_share + extra_row_count).astype(jnp.int32)


def with_ends(array, own_key, smallest, top_value):
    longest = array.shape.index(max(array.shape))
    spots = []
    for shift in (0, 1):
        where = [jax.random.randint(jax.random.fold_in(own_key, axis), (), 0, length) for axis, length in enumerate(array.shape)]
        where[longest] = (where[longest] + shift) % array.shape[longest]
        spots.append(tuple(where))
    return array.at[spots[0]].set(smallest).at[spots[1]].set(top_value)


def shard_levels(key, extent, cuts, least, high):
    factor_of, own = 1.0, jax.random.fold_in(key, 6)
    for dim, blocks in cuts:
        heights = jnp.exp(jax.random.uniform(jax.random.fold_in(own, dim), (blocks,), jnp.float32, least / len(cuts), high / len(cuts)))
        factor_of = factor_of * jnp.repeat(heights, extent[dim] // blocks).reshape([-1 if axis == dim else 1 for axis in range(len(extent))])
    return factor_of


def rank_bounds(amount, skew):
    weights = [(1 << 20) // math.isqrt(grade ** skew) + 1 for grade in range(1, amount + 1)]
    scale = 1 + sum(weights) // (1 << 30)
    return np.cumsum(np.array([max(1, weight // scale) for weight in weights]))


def ranked(own_key, dims, number_of, slope):
    table = rank_bounds(number_of, slope)
    lot = jax.random.randint(jax.random.fold_in(own_key, 1), dims, 0, int(table[number_of - 1]))
    grade = jnp.searchsorted(jnp.asarray(table, jnp.int32), lot, side="right")
    return jax.random.permutation(jax.random.fold_in(own_key, 2), number_of)[grade].astype(jnp.int32)


def centred(own_key, extent, scale, limit, cuts=(), held_as=jnp.bfloat16):
    factor_of = shard_levels(own_key, extent, cuts, -0.22, 0.18) if cuts else 1.0
    values = jax.random.normal(own_key, extent, jnp.float32) * scale * factor_of
    return jnp.minimum(jnp.maximum(values, -limit), limit).astype(held_as)


def setup_inputs(seed: int = 0) -> dict:
    arg_keys = jax.random.split(jax.random.key(seed), 5)
    return {
        "vectors": centred(arg_keys[0], (ROWS, D), 1.0, 6.0, ((0, 128),)),
        "parents": with_ends(jax.random.randint(arg_keys[1], (ROWS,), 0, PAR_GRP), jax.random.fold_in(arg_keys[1], 1), 0, PAR_GRP - 1).astype(jnp.int32),
        "children": with_ends(ranked(arg_keys[2], (ROWS,), CHILD, 1), jax.random.fold_in(arg_keys[2], 3), 0, CHILD - 1).astype(jnp.int32),
        "counts": draw_counts(jax.random.fold_in(arg_keys[4], 71), 0),
    }


def pick_parent(all_dists, row_codes):
    row_count = all_dists.shape[0]
    stacked = all_dists.reshape(row_count, PAR_GRP, CHILD)
    parent_ids = jnp.maximum(row_codes, 0) // CHILD
    chosen = parent_ids[:, None, None] == jnp.arange(PAR_GRP, dtype=jnp.int32)[None, :, None]
    picked = jnp.sum(jnp.where(chosen, stacked, jnp.zeros((), jnp.float32)), axis=1)
    return jnp.where(row_codes[:, None] >= 0, picked, jnp.zeros((), jnp.float32))


def column_block(centroids, vec_norm, arrived):
    cent_wide = centroids.astype(jnp.float32)
    cent_norm = jnp.sum(cent_wide * cent_wide, axis=1)
    cross = jnp.dot(arrived, centroids.T, preferred_element_type=jnp.float32)
    return (vec_norm[:, None] - 2.0 * cross + cent_norm[None, :]) / D


def reference(vectors, parents, children, counts):
    shards = N_GRP * N_MEM
    width = PAR_GRP * CHILD
    stored = vectors.reshape(shards, VEC_DEV, D)
    parent_rows = parents.reshape(shards, VEC_DEV)
    child_rows = children.reshape(shards, VEC_DEV)
    offsets = (jnp.cumsum(counts, axis=1) - counts).astype(jnp.int32)
    slots = jnp.arange(SHARD_GROUP_SLOTS, dtype=jnp.int32)
    filled = slots[None, None, :] < counts[:, :, None]
    source_rows = jnp.where(filled, offsets[:, :, None] + slots[None, None, :], 0).astype(jnp.int32)
    flat_rows = source_rows.reshape(shards, N_GRP * SHARD_GROUP_SLOTS)
    flat_filled = filled.reshape(shards, N_GRP * SHARD_GROUP_SLOTS)
    sent = jnp.take_along_axis(stored, flat_rows[:, :, None], axis=1)
    sent = jnp.where(flat_filled[:, :, None], sent, jnp.zeros((), jnp.bfloat16))
    row_codes = jnp.take_along_axis(parent_rows, flat_rows, axis=1) * CHILD + jnp.take_along_axis(child_rows, flat_rows, axis=1)
    row_codes = jnp.where(flat_filled, row_codes, -1).astype(jnp.int32)
    sent = sent.reshape(N_GRP, N_MEM, N_GRP, SHARD_GROUP_SLOTS, D).transpose(2, 1, 0, 3, 4).reshape(N_GRP, N_MEM * N_GRP * SHARD_GROUP_SLOTS, D)
    row_codes = row_codes.reshape(N_GRP, N_MEM, N_GRP, SHARD_GROUP_SLOTS).transpose(2, 1, 0, 3).reshape(N_GRP, N_MEM * N_GRP * SHARD_GROUP_SLOTS)

    def one_group(paired):
        arrived, arrived_codes = paired
        segment_ids = jnp.where(arrived_codes >= 0, arrived_codes, width).astype(jnp.int32)
        vec_wide = arrived.astype(jnp.float32)
        child_sums = jax.ops.segment_sum(vec_wide, segment_ids, num_segments=width + 1)[:width]
        child_counts = jax.ops.segment_sum(jnp.ones(arrived_codes.shape, jnp.float32), segment_ids, num_segments=width + 1)[:width]
        centroids = (child_sums / jnp.maximum(child_counts, 1.0)[:, None]).astype(jnp.bfloat16)
        vec_norm = jnp.sum(vec_wide * vec_wide, axis=1)
        return pick_parent(column_block(centroids, vec_norm, arrived), arrived_codes)

    result = lax.map(one_group, (sent, row_codes))
    return result.reshape(N_GRP * N_MEM * N_GRP * SHARD_GROUP_SLOTS, CHILD)
```

```python
import functools

import jax
import jax.numpy as jnp
from jax import lax
from jax.experimental import pallas as pl
from jax.experimental.pallas import tpu as pltpu
from jax.sharding import PartitionSpec as P

D = 768
CHILD = 1024
PAR_GRP = 2
CODES = PAR_GRP * CHILD
GROUPS = 8
SLOTS = 256
MEMBERS = 16
OWNED = CODES // MEMBERS
ROWS_DEV = 1024
EXTRA = 16
LANES = 128
WIDTHS = (768,)

BF = jnp.bfloat16
F32 = jnp.float32
WHOLE = pl.BlockSpec(memory_space=pltpu.VMEM)


def cost(flops, nbytes):
    return pl.CostEstimate(flops=int(flops), bytes_accessed=int(nbytes), transcendentals=0)


def pack_kernel(start, width, with_codes, counts_ref, vec_ref, par_ref, chi_ref, out_ref, wide_ref):
    for j in range(width // LANES):
        at = start + j * LANES
        wide_ref[j, 0:ROWS_DEV, :] = vec_ref[:, at:at + LANES].astype(F32)
        wide_ref[j, ROWS_DEV:ROWS_DEV + SLOTS, :] = jnp.zeros((SLOTS, LANES), F32)
    offset = 0
    if with_codes:
        codes = par_ref[...] * CHILD + chi_ref[...]
        slot = lax.broadcasted_iota(jnp.int32, (1, SLOTS), 1)
        line = lax.broadcasted_iota(jnp.int32, (EXTRA, SLOTS), 0)
    for h in range(GROUPS):
        filled = counts_ref[0, h]
        for j in range(width // LANES):
            out_ref[h, 0:SLOTS, j * LANES:(j + 1) * LANES] = wide_ref[j, pl.ds(offset, SLOTS), :].astype(BF)
        if with_codes:
            mine = codes if h == 0 else pltpu.roll(codes, lax.rem(ROWS_DEV - offset, ROWS_DEV), 1)
            mine = mine[:, :SLOTS]
            mine = jnp.where(slot < filled, mine, -1)
            high = jnp.broadcast_to((mine >> 7).astype(F32), (EXTRA, SLOTS))
            low = jnp.broadcast_to((mine & 127).astype(F32), (EXTRA, SLOTS))
            block = jnp.where(line == 0, high, jnp.where(line == 1, low, 0.0))
            out_ref[h, SLOTS:SLOTS + EXTRA, 0:SLOTS] = block.astype(BF)
            if width > SLOTS:
                out_ref[h, SLOTS:SLOTS + EXTRA, SLOTS:width] = jnp.zeros((EXTRA, width - SLOTS), BF)
        offset = offset + filled


def pack(start, width, with_codes, counts, vectors, parents, children):
    rows = SLOTS + (EXTRA if with_codes else 0)
    return pl.pallas_call(
        functools.partial(pack_kernel, start, width, with_codes),
        out_shape=jax.ShapeDtypeStruct((GROUPS, rows, width), BF),
        in_specs=[pl.BlockSpec(memory_space=pltpu.SMEM), WHOLE, WHOLE, WHOLE],
        out_specs=WHOLE,
        scratch_shapes=[pltpu.VMEM((width // LANES, ROWS_DEV + SLOTS, LANES), F32)],
        cost_estimate=cost(1e6, ROWS_DEV * width * 6),
        name="pack",
    )(counts, vectors, parents, children)


def codes_of(block):
    wide = block.astype(F32)
    return (wide[0:1, :] * 128.0 + wide[1:2, :]).astype(jnp.int32)


def sums_kernel(with_counts, codes_ref, rows_ref, out_ref):
    first = pl.program_id(0) * (2 * OWNED)
    child = lax.broadcasted_iota(jnp.int32, (2 * OWNED, SLOTS), 0) + first
    total = None
    tally = None
    for s in range(GROUPS):
        hit = child == codes_of(codes_ref[s, :, 0:SLOTS])
        onehot = jnp.where(hit, 1.0, 0.0).astype(BF)
        part = jnp.dot(onehot, rows_ref[s, 0:SLOTS, :], preferred_element_type=F32)
        total = part if total is None else total + part
        if with_counts:
            here = lax.dot_general(
                jnp.ones((EXTRA, SLOTS), BF), onehot, (((1,), (1,)), ((), ())), preferred_element_type=F32
            )
            tally = here if tally is None else tally + here
    for k in range(2):
        out_ref[k, 0:OWNED, :] = total[k * OWNED:(k + 1) * OWNED].astype(BF)
        if with_counts:
            width = out_ref.shape[2]
            mine = tally[:, k * OWNED:(k + 1) * OWNED]
            high = jnp.floor(mine * (1.0 / 128.0))
            low = mine - high * 128.0
            line = lax.broadcasted_iota(jnp.int32, (EXTRA, OWNED), 0)
            block = jnp.where(line == 0, high, jnp.where(line == 1, low, 0.0))
            out_ref[k, OWNED:OWNED + EXTRA, 0:OWNED] = block.astype(BF)
            out_ref[k, OWNED:OWNED + EXTRA, OWNED:width] = jnp.zeros((EXTRA, width - OWNED), BF)


def sums(with_counts, carrier, rows):
    width = rows.shape[2]
    lines = OWNED + (EXTRA if with_counts else 0)
    return pl.pallas_call(
        functools.partial(sums_kernel, with_counts),
        grid=(MEMBERS // 2,),
        out_shape=jax.ShapeDtypeStruct((MEMBERS, lines, width), BF),
        in_specs=[
            pl.BlockSpec((GROUPS, EXTRA, SLOTS), lambda i: (0, SLOTS // EXTRA, 0), pipeline_mode=pl.Buffered(1)),
            pl.BlockSpec((GROUPS, rows.shape[1], width), lambda i: (0, 0, 0), pipeline_mode=pl.Buffered(1)),
        ],
        out_specs=pl.BlockSpec((2, lines, width), lambda i: (i, 0, 0)),
        cost_estimate=cost(2 * CODES * GROUPS * SLOTS * width, 4 * CODES * width),
        name="sums",
    )(carrier, rows)


def mean_kernel(first, parts_ref, count_ref, out_ref, *rest):
    total = parts_ref[0, 0:OWNED, :].astype(F32)
    for m in range(1, MEMBERS):
        total = total + parts_ref[m, 0:OWNED, :].astype(F32)
    if first:
        tally = jnp.zeros((1, OWNED), F32)
        for m in range(MEMBERS):
            block = parts_ref[m, OWNED:OWNED + EXTRA, 0:OWNED].astype(F32)
            tally = tally + block[0:1, :] * 128.0 + block[1:2, :]
        row = lax.broadcasted_iota(jnp.int32, (OWNED, OWNED), 0)
        col = lax.broadcasted_iota(jnp.int32, (OWNED, OWNED), 1)
        spread = jnp.where(row == col, jnp.broadcast_to(tally, (OWNED, OWNED)), 0.0)
        count = jnp.maximum(jnp.sum(spread, axis=1, keepdims=True), 1.0)
        rest[0][...] = jnp.broadcast_to(count, (OWNED, OWNED))
    else:
        count = count_ref[:, 0:1]
    mean = (total / count).astype(BF)
    for m in range(MEMBERS):
        out_ref[m] = mean


def mean(parts, counts):
    first = counts is None
    width = parts.shape[2]
    out = [jax.ShapeDtypeStruct((MEMBERS, OWNED, width), BF)]
    if first:
        out.append(jax.ShapeDtypeStruct((OWNED, OWNED), F32))
        counts = jnp.zeros((8, 128), F32)
    got = pl.pallas_call(
        functools.partial(mean_kernel, first),
        out_shape=out,
        in_specs=[WHOLE, WHOLE],
        out_specs=[WHOLE] * len(out),
        cost_estimate=cost(2 * CODES * width, 4 * CODES * width),
        name="mean",
    )(parts, counts)
    return (got[0], got[1]) if first else (got[0], counts)


def dist_kernel(first, last, codes_ref, rows_ref, cent_ref, *rest):
    if first:
        out_ref, square_ref = rest
    else:
        old_ref, out_ref, square_ref = rest
    width = rows_ref.shape[2]

    @pl.when(pl.program_id(0) == 0)
    def _():
        for m in range(MEMBERS):
            wide = cent_ref[m].astype(F32)
            wide = wide * wide
            fold = wide[:, 0:128]
            for k in range(1, width // 128):
                fold = fold + wide[:, k * 128:(k + 1) * 128]
            square_ref[:, m * OWNED:(m + 1) * OWNED] = jnp.broadcast_to(
                jnp.sum(fold.T, axis=0, keepdims=True), (8, OWNED)
            )

    code = jnp.broadcast_to(codes_of(codes_ref[0, :, 0:SLOTS]), (128, SLOTS))
    code = code.astype(F32).T[:, 0:1]
    rows = rows_ref[0, 0:SLOTS, :]
    wide = rows.astype(F32)
    norm = jnp.sum(wide * wide, axis=1, keepdims=True)
    upper = code >= float(CHILD)
    zero = jnp.zeros_like(rows)
    rows0 = jnp.where(upper, zero, rows)
    rows1 = jnp.where(upper, rows, zero)
    half = MEMBERS // PAR_GRP
    cent0 = cent_ref[0:half].reshape(CHILD, width)
    cent1 = cent_ref[half:MEMBERS].reshape(CHILD, width)
    over_k = (((1,), (1,)), ((), ()))
    cross = lax.dot_general(rows0, cent0, over_k, preferred_element_type=F32)
    cross = cross + lax.dot_general(rows1, cent1, over_k, preferred_element_type=F32)
    square = jnp.where(upper, square_ref[0:1, CHILD:CODES], square_ref[0:1, 0:CHILD])
    value = norm + square - 2.0 * cross
    if not first:
        value = value + old_ref[...]
    if last:
        value = jnp.where(code >= 0.0, value * (1.0 / D), 0.0)
    out_ref[...] = value


def dist(first, last, carrier, rows, cent, old):
    width = rows.shape[2]
    in_specs = [
        pl.BlockSpec((1, EXTRA, SLOTS), lambda i: (i, SLOTS // EXTRA, 0)),
        pl.BlockSpec((1, rows.shape[1], width), lambda i: (i, 0, 0)),
        pl.BlockSpec((MEMBERS, OWNED, width), lambda i: (0, 0, 0), pipeline_mode=pl.Buffered(1)),
    ]
    args = [carrier, rows, cent]
    if not first:
        in_specs.append(pl.BlockSpec((SLOTS, CHILD), lambda i: (i, 0)))
        args.append(old)
    return pl.pallas_call(
        functools.partial(dist_kernel, first, last),
        grid=(GROUPS,),
        out_shape=jax.ShapeDtypeStruct((GROUPS * SLOTS, CHILD), F32),
        in_specs=in_specs,
        out_specs=pl.BlockSpec((SLOTS, CHILD), lambda i: (i, 0)),
        scratch_shapes=[pltpu.VMEM((8, CODES), F32)],
        cost_estimate=cost(2 * CODES * GROUPS * SLOTS * width, 8 * GROUPS * SLOTS * CHILD),
        name="dist",
    )(*args)


def swap(x, axis):
    return lax.all_to_all(x, axis, split_axis=0, concat_axis=0, tiled=True)


def body(vectors, parents, children, counts):
    parents = parents.reshape(1, ROWS_DEV)
    children = children.reshape(1, ROWS_DEV)
    starts = [sum(WIDTHS[:k]) for k in range(len(WIDTHS))]
    arrived = [
        swap(pack(at, width, k == 0, counts, vectors, parents, children), "grp")
        for k, (at, width) in enumerate(zip(starts, WIDTHS))
    ]
    carrier = arrived[0]
    parts = [swap(sums(k == 0, carrier, rows), "mem") for k, rows in enumerate(arrived)]
    tally = None
    cents = []
    for part in parts:
        own, tally = mean(part, tally)
        cents.append(swap(own, "mem"))
    out = None
    for k, (rows, cent) in enumerate(zip(arrived, cents)):
        out = dist(k == 0, k == len(WIDTHS) - 1, carrier, rows, cent, out)
    return out


def solution(mesh):
    in_specs = (
        P(("grp", "mem"), None),
        P(("grp", "mem")),
        P(("grp", "mem")),
        P(("grp", "mem"), None),
    )
    out_specs = P(("grp", "mem"), None)
    return jax.shard_map(body, mesh=mesh, in_specs=in_specs, out_specs=out_specs, check_vma=False)
```

```python
import functools

import jax
import jax.numpy as jnp
from jax import lax
from jax.experimental import pallas as pl
from jax.experimental.pallas import tpu as pltpu
from jax.sharding import PartitionSpec as P

D = 768
CHILD = 1024
GROUPS = 8
SLOTS = 256
ROWS_DEV = 1024
LANES = 128
SIDE = 4
TILE = CHILD // SIDE
EXTRA = 8
LINES = TILE + EXTRA

BF = jnp.bfloat16
F32 = jnp.float32
I32 = jnp.int32
WHOLE = pl.BlockSpec(memory_space=pltpu.VMEM)
ANY = pl.BlockSpec(memory_space=pl.ANY)

RELATIVE = ((0, 0), (0, 1), (1, 0), (1, 1), (3, 0), (3, 1), (2, 0), (2, 1))
STAGES = ((0, 1), (2, 3, 4, 5), (6, 7))
STEPS = (1, 3, 2)


def cost(flops, nbytes):
    return pl.CostEstimate(flops=int(flops), bytes_accessed=int(nbytes), transcendentals=0)


def vmem(mib):
    return pltpu.CompilerParams(vmem_limit_bytes=mib << 20)


def block_shape():
    return jax.ShapeDtypeStruct((LINES, D), BF)


def split_rows(values, width):
    high = jnp.floor(values * (1.0 / 128.0))
    low = values - high * 128.0
    line = lax.broadcasted_iota(I32, (EXTRA, width), 0)
    return jnp.where(line == 0, high, jnp.where(line == 1, low, 0.0)).astype(BF)


def joined_rows(block):
    wide = block.astype(F32)
    return wide[0:1, :] * 128.0 + wide[1:2, :]


def pack_kernel(counts_ref, vec_ref, par_ref, chi_ref, *rest):
    outs, (wide_ref, offset_ref) = rest[:GROUPS], rest[GROUPS:]
    me = lax.axis_index("grp")
    offset = 0
    for h in range(GROUPS):
        offset_ref[h] = offset
        offset = offset + counts_ref[0, h]
    for j in range(D // LANES):
        wide_ref[j, 0:ROWS_DEV, :] = vec_ref[:, j * LANES:(j + 1) * LANES].astype(F32)
        wide_ref[j, ROWS_DEV:ROWS_DEV + SLOTS, :] = jnp.zeros((SLOTS, LANES), F32)
    codes = par_ref[...] * CHILD + chi_ref[...]
    slot = lax.broadcasted_iota(I32, (1, SLOTS), 1)
    for k, (dy, dc) in enumerate(RELATIVE):
        core = lax.rem(me, 2)
        core = 1 - core if dc else core
        h = lax.rem(lax.div(me, 2) + dy, SIDE) * 2 + core
        start = offset_ref[h]
        filled = counts_ref[0, h]
        for j in range(D // LANES):
            outs[k][0:SLOTS, j * LANES:(j + 1) * LANES] = wide_ref[j, pl.ds(start, SLOTS), :].astype(BF)
        mine = pltpu.roll(codes, lax.rem(ROWS_DEV - start, ROWS_DEV), 1)[:, :SLOTS]
        mine = jnp.where(slot < filled, mine, -1).astype(F32)
        outs[k][SLOTS:LINES, 0:SLOTS] = split_rows(mine, SLOTS)
        outs[k][SLOTS:LINES, SLOTS:D] = jnp.zeros((EXTRA, D - SLOTS), BF)


def pack(counts, vectors, parents, children):
    return pl.pallas_call(
        pack_kernel,
        out_shape=[block_shape()] * GROUPS,
        in_specs=[pl.BlockSpec(memory_space=pltpu.SMEM), WHOLE, WHOLE, WHOLE],
        out_specs=[WHOLE] * GROUPS,
        scratch_shapes=[
            pltpu.VMEM((D // LANES, ROWS_DEV + SLOTS, LANES), F32),
            pltpu.SMEM((GROUPS,), I32),
        ],
        cost_estimate=cost(1e6, 3 * GROUPS * LINES * D),
        compiler_params=vmem(16),
        name="pack",
    )(counts, vectors, parents, children)


def sums_kernel(stage, *refs):
    first, last = stage == 0, stage == len(STAGES) - 1
    here = STAGES[stage]
    n = len(here)
    refs = list(refs)
    blocks = [refs.pop(0) for _ in range(n)]
    if not first:
        old_ref = refs.pop(0)
        refs.pop(0)
    rows_ref = refs.pop(0)
    outs = [refs.pop(0) for _ in range(2 * SIDE)] if last else [refs.pop(0)] * (2 * SIDE)
    buf_ref, total_ref, in_sem, row_sem, old_sem, out_sem = refs[:6]
    done_ref = refs[6] if last else total_ref

    me = lax.axis_index("grp")
    place = lax.axis_index("mem")
    z, x = lax.div(place, SIDE), lax.rem(place, SIDE)
    loads = [pltpu.make_async_copy(blocks[j], buf_ref.at[j], in_sem.at[j]) for j in range(n)]
    for c in loads:
        c.start()
    olds = []
    if not first:
        olds = [pltpu.make_async_copy(old_ref.at[t], total_ref.at[t], old_sem.at[t]) for t in range(2 * SIDE)]
        for c in olds:
            c.start()
    for c in loads:
        c.wait()
    keeps = []
    for j, k in enumerate(here):
        dy, dc = RELATIVE[k]
        core = lax.rem(me, 2)
        core = 1 - core if dc else core
        source = lax.rem(lax.div(me, 2) + SIDE - dy, SIDE) * 2 + core
        keeps.append(pltpu.make_async_copy(buf_ref.at[j], rows_ref.at[source], row_sem.at[j]))
        keeps[-1].start()
    codes = [joined_rows(buf_ref[j, SLOTS:LINES, 0:SLOTS]).astype(I32) for j in range(n)]
    line = lax.broadcasted_iota(I32, (TILE, SLOTS), 0)
    sends = []
    for t in range(2 * SIDE):
        k = t % SIDE
        base = lax.rem(x + k, SIDE) * TILE if t < SIDE else lax.rem(z + k, SIDE) * TILE + CHILD
        total = None
        tally = None
        for j in range(n):
            onehot = jnp.where(line == codes[j] - base, 1.0, 0.0).astype(BF)
            part = jnp.dot(onehot, buf_ref[j, 0:SLOTS, :], preferred_element_type=F32)
            count = lax.dot_general(
                jnp.ones((EXTRA, SLOTS), BF), onehot, (((1,), (1,)), ((), ())), preferred_element_type=F32
            )
            total = part if total is None else total + part
            tally = count if tally is None else tally + count
        if not first:
            olds[t].wait()
            total = total + total_ref[t, 0:TILE, :]
            tally = tally + total_ref[t, TILE:LINES, 0:TILE]
        if last:
            done_ref[t, 0:TILE, :] = total.astype(BF)
            done_ref[t, TILE:LINES, 0:TILE] = split_rows(tally[0:1, :], TILE)
            done_ref[t, TILE:LINES, TILE:D] = jnp.zeros((EXTRA, D - TILE), BF)
            sends.append(pltpu.make_async_copy(done_ref.at[t], outs[t], out_sem.at[t]))
        else:
            total_ref[t, 0:TILE, :] = total
            total_ref[t, TILE:LINES, 0:TILE] = tally
            sends.append(pltpu.make_async_copy(total_ref.at[t], outs[t].at[t], out_sem.at[t]))
        sends[-1].start()
    for c in keeps + sends:
        c.wait()


def sums(stage, blocks, old, rows):
    first, last = stage == 0, stage == len(STAGES) - 1
    n = len(blocks)
    kept = jax.ShapeDtypeStruct((GROUPS, LINES, D), BF)
    tiles = jax.ShapeDtypeStruct((2 * SIDE, LINES, D), F32)
    args = list(blocks)
    aliases = {}
    if not first:
        args += [old, rows]
        aliases = {n + 1: 0} if last else {n + 1: 0, n: 1}
    out_shape = [kept] + ([block_shape()] * (2 * SIDE) if last else [tiles])
    scratch = [
        pltpu.VMEM((n, LINES, D), BF),
        pltpu.VMEM((2 * SIDE, LINES, D), F32),
        pltpu.SemaphoreType.DMA((n,)),
        pltpu.SemaphoreType.DMA((n,)),
        pltpu.SemaphoreType.DMA((2 * SIDE,)),
        pltpu.SemaphoreType.DMA((2 * SIDE,)),
    ]
    if last:
        scratch.append(pltpu.VMEM((2 * SIDE, LINES, D), BF))
    return pl.pallas_call(
        functools.partial(sums_kernel, stage),
        out_shape=out_shape,
        in_specs=[ANY] * len(args),
        out_specs=[ANY] * len(out_shape),
        scratch_shapes=scratch,
        input_output_aliases=aliases,
        cost_estimate=cost(4 * CHILD * n * SLOTS * D, 12 * CHILD * D),
        compiler_params=vmem(24),
        name="sums",
    )(*args)


def total_of(parts):
    total = parts[0][0:TILE, :].astype(F32)
    tally = joined_rows(parts[0][TILE:LINES, 0:TILE])
    for part in parts[1:]:
        total = total + part[0:TILE, :].astype(F32)
        tally = tally + joined_rows(part[TILE:LINES, 0:TILE])
    return total, tally


def partial_kernel(a_ref, b_ref, c_ref, d_ref, out_ref):
    total, tally = total_of((a_ref, b_ref, c_ref, d_ref))
    out_ref[0:TILE, :] = total.astype(BF)
    out_ref[TILE:LINES, 0:TILE] = split_rows(tally, TILE)
    out_ref[TILE:LINES, TILE:D] = jnp.zeros((EXTRA, D - TILE), BF)


def mean_kernel(a_ref, b_ref, c_ref, d_ref, out_ref):
    total, tally = total_of((a_ref, b_ref, c_ref, d_ref))
    count = jnp.maximum(jnp.broadcast_to(tally, (LANES, TILE)).T[:, 0:1], 1.0)
    out_ref[...] = (total / count).astype(BF)


def reduce_four(kernel, name, lines, parts):
    return pl.pallas_call(
        kernel,
        out_shape=jax.ShapeDtypeStruct((lines, D), BF),
        in_specs=[WHOLE] * SIDE,
        out_specs=WHOLE,
        cost_estimate=cost(4 * TILE * D, 10 * TILE * D),
        compiler_params=vmem(8),
        name=name,
    )(*parts)


def row_facts(code_block, rows):
    code = jnp.broadcast_to(joined_rows(code_block), (LANES, SLOTS)).T[:, 0:1]
    wide = rows.astype(F32)
    norm = jnp.sum(wide * wide, axis=1, keepdims=True) * (1.0 / D)
    return norm, jnp.logical_and(code >= 0.0, code < float(CHILD)), code >= float(CHILD)


def square_row(cent_ref):
    wide = cent_ref[...].astype(F32)
    wide = wide * wide
    fold = wide[:, 0:LANES]
    for k in range(1, D // LANES):
        fold = fold + wide[:, k * LANES:(k + 1) * LANES]
    return jnp.broadcast_to(jnp.sum(fold.T, axis=0, keepdims=True) * (1.0 / D), (8, TILE))


def against(rows, cent_ref, norm, square):
    cross = lax.dot_general(rows, cent_ref[...], (((1,), (1,)), ((), ())), preferred_element_type=F32)
    return norm + square - cross * (2.0 / D)


def near_kernel(rows_ref, *refs):
    near = (0,) + STEPS[:2]
    cents = refs[:2 * len(near)]
    out_ref, square_ref = refs[2 * len(near):]
    place = lax.axis_index("mem")
    z, x = lax.div(place, SIDE), lax.rem(place, SIDE)

    @pl.when(pl.program_id(0) == 0)
    def _():
        for n, cent in enumerate(cents):
            square_ref[n] = square_row(cent)

    rows = rows_ref[0, 0:SLOTS, :]
    norm, lower, upper = row_facts(rows_ref[0, SLOTS:LINES, 0:SLOTS], rows)

    def columns(spot, k):
        return pl.ds(pl.multiple_of(lax.rem(spot + SIDE - k, SIDE) * TILE, TILE), TILE)

    out_ref[:, columns(x, 2)] = jnp.zeros((SLOTS, TILE), F32)
    for n, k in enumerate(near):
        value = against(rows, cents[n], norm, square_ref[n, 0:1, :])
        out_ref[:, columns(x, k)] = jnp.where(lower, value, 0.0)
    for n, k in enumerate(near):
        m = n + len(near)
        value = against(rows, cents[m], norm, square_ref[m, 0:1, :])
        at = columns(z, k)
        out_ref[:, at] = jnp.where(upper, value, out_ref[:, at])


def near(rows, cents):
    return pl.pallas_call(
        near_kernel,
        grid=(GROUPS,),
        out_shape=jax.ShapeDtypeStruct((GROUPS * SLOTS, CHILD), F32),
        in_specs=[pl.BlockSpec((1, LINES, D), lambda i: (i, 0, 0))] + [WHOLE] * len(cents),
        out_specs=pl.BlockSpec((SLOTS, CHILD), lambda i: (i, 0)),
        scratch_shapes=[pltpu.VMEM((len(cents), 8, TILE), F32)],
        cost_estimate=cost(3 * CHILD * GROUPS * SLOTS * D, 4 * GROUPS * SLOTS * CHILD),
        compiler_params=vmem(24),
        name="near",
    )(rows, *cents)


def far_kernel(spot_ref, rows_ref, low_ref, high_ref, old_ref, out_ref, square_ref):
    part, i = pl.program_id(0), pl.program_id(1)

    @pl.when(jnp.logical_and(part == 0, i == 0))
    def _():
        square_ref[0] = square_row(low_ref)
        square_ref[1] = square_row(high_ref)

    rows = rows_ref[0, 0:SLOTS, :]
    norm, lower, upper = row_facts(rows_ref[0, SLOTS:LINES, 0:SLOTS], rows)

    @pl.when(part == 0)
    def _():
        value = against(rows, low_ref, norm, square_ref[0, 0:1, :])
        out_ref[...] = jnp.where(lower, value, old_ref[...])

    @pl.when(part == 1)
    def _():
        value = against(rows, high_ref, norm, square_ref[1, 0:1, :])
        out_ref[...] = jnp.where(upper, value, old_ref[...])


def far(spots, rows, low, high, old):
    return pl.pallas_call(
        far_kernel,
        grid_spec=pltpu.PrefetchScalarGridSpec(
            num_scalar_prefetch=1,
            grid=(2, GROUPS),
            in_specs=[
                pl.BlockSpec((1, LINES, D), lambda p, i, s: (i, 0, 0)),
                WHOLE,
                WHOLE,
                pl.BlockSpec((SLOTS, TILE), lambda p, i, s: (i, s[p])),
            ],
            out_specs=pl.BlockSpec((SLOTS, TILE), lambda p, i, s: (i, s[p])),
            scratch_shapes=[pltpu.VMEM((2, 8, TILE), F32)],
        ),
        out_shape=jax.ShapeDtypeStruct((GROUPS * SLOTS, CHILD), F32),
        input_output_aliases={4: 0},
        cost_estimate=cost(CHILD * GROUPS * SLOTS * D, 4 * GROUPS * SLOTS * CHILD),
        compiler_params=vmem(16),
        name="far",
    )(spots, rows, low, high, old)


def along_grp(dy, dc):
    return [(y * 2 + c, ((y + dy) % SIDE) * 2 + (c ^ dc)) for y in range(SIDE) for c in range(2)]


def along_x(k):
    return [(z * SIDE + x, z * SIDE + (x + k) % SIDE) for z in range(SIDE) for x in range(SIDE)]


def along_z(k):
    return [(z * SIDE + x, ((z + k) % SIDE) * SIDE + x) for z in range(SIDE) for x in range(SIDE)]


def both(low, high, first, second):
    got_low, got_high = {}, {}
    for k in STEPS:
        got_low[k] = lax.ppermute(low[k], "mem", first(k))
        got_high[k] = lax.ppermute(high[k], "mem", second(k))
    return got_low, got_high


def body(vectors, parents, children, counts):
    parents = parents.reshape(1, ROWS_DEV)
    children = children.reshape(1, ROWS_DEV)
    packed = pack(counts, vectors, parents, children)
    arrived = [
        block if step == (0, 0) else lax.ppermute(block, "grp", along_grp(*step))
        for block, step in zip(packed, RELATIVE)
    ]
    rows, tiles = None, [None]
    for stage, here in enumerate(STAGES):
        rows, *tiles = sums(stage, [arrived[k] for k in here], tiles[0], rows)
    low, high = tiles[:SIDE], tiles[SIDE:]

    got_low, got_high = both(low, high, along_x, along_z)
    low = reduce_four(partial_kernel, "partial", LINES, [low[0]] + [got_low[k] for k in STEPS])
    high = reduce_four(partial_kernel, "partial", LINES, [high[0]] + [got_high[k] for k in STEPS])

    got_low, got_high = both([low] * SIDE, [high] * SIDE, along_z, along_x)
    low = reduce_four(mean_kernel, "mean", TILE, [low] + [got_low[k] for k in STEPS])
    high = reduce_four(mean_kernel, "mean", TILE, [high] + [got_high[k] for k in STEPS])

    got_low, got_high = both([low] * SIDE, [high] * SIDE, along_x, along_z)
    out = near(rows, [low] + [got_low[k] for k in STEPS[:2]] + [high] + [got_high[k] for k in STEPS[:2]])
    place = lax.axis_index("mem")
    spots = jnp.stack([lax.rem(lax.rem(place, SIDE) + 2, SIDE), lax.rem(lax.div(place, SIDE) + 2, SIDE)])
    return far(spots, rows, got_low[2], got_high[2], out)


def solution(mesh):
    in_specs = (
        P(("grp", "mem"), None),
        P(("grp", "mem")),
        P(("grp", "mem")),
        P(("grp", "mem"), None),
    )
    out_specs = P(("grp", "mem"), None)
    return jax.shard_map(body, mesh=mesh, in_specs=in_specs, out_specs=out_specs, check_vma=False)
```

```python
import functools

import jax
import jax.numpy as jnp
from jax import lax
from jax.experimental import pallas as pl
from jax.experimental.pallas import tpu as pltpu
from jax.sharding import PartitionSpec as P

D = 768
CHILD = 1024
GROUPS = 8
SLOTS = 256
ROWS_DEV = 1024
LANES = 128
SIDE = 4
TILE = CHILD // SIDE
EXTRA = 8
LINES = TILE + EXTRA

BF = jnp.bfloat16
F32 = jnp.float32
I32 = jnp.int32
WHOLE = pl.BlockSpec(memory_space=pltpu.VMEM)

RELATIVE = ((0, 0), (0, 1), (1, 0), (1, 1), (3, 0), (3, 1), (2, 0), (2, 1))
STAGES = ((0, 1), (2, 4), (3, 5, 6, 7))
STEPS = (1, 3, 2)


def cost(flops, nbytes):
    return pl.CostEstimate(flops=int(flops), bytes_accessed=int(nbytes), transcendentals=0)


def vmem(mib):
    return pltpu.CompilerParams(vmem_limit_bytes=mib << 20)


def block_shape():
    return jax.ShapeDtypeStruct((LINES, D), BF)


def split_rows(values, width):
    high = jnp.floor(values * (1.0 / 128.0))
    low = values - high * 128.0
    line = lax.broadcasted_iota(I32, (EXTRA, width), 0)
    return jnp.where(line == 0, high, jnp.where(line == 1, low, 0.0)).astype(BF)


def joined_rows(block):
    wide = block.astype(F32)
    return wide[0:1, :] * 128.0 + wide[1:2, :]


def pack_kernel(counts_hbm, vec_hbm, par_hbm, chi_hbm, *rest):
    outs, (counts_ref, vec_ref, ids_ref, wide_ref, done_ref, offset_ref, sems, out_sems) = rest[:GROUPS], rest[GROUPS:]
    me = lax.axis_index("grp")
    small = [
        pltpu.make_async_copy(counts_hbm, counts_ref, sems.at[0]),
        pltpu.make_async_copy(par_hbm, ids_ref.at[0], sems.at[1]),
        pltpu.make_async_copy(chi_hbm, ids_ref.at[1], sems.at[2]),
    ]
    parts = [pl.ds(n * SLOTS, SLOTS) for n in range(ROWS_DEV // SLOTS)]
    loads = [pltpu.make_async_copy(vec_hbm.at[p], vec_ref.at[p], sems.at[3 + n]) for n, p in enumerate(parts)]
    for c in small + loads:
        c.start()
    for j in range(D // LANES):
        wide_ref[j, ROWS_DEV:ROWS_DEV + SLOTS, :] = jnp.zeros((SLOTS, LANES), F32)
    for c in small:
        c.wait()
    offset = 0
    for h in range(GROUPS):
        offset_ref[h] = offset
        offset = offset + counts_ref[0, h]
    codes = ids_ref[0] * CHILD + ids_ref[1]
    slot = lax.broadcasted_iota(I32, (1, SLOTS), 1)
    spots = []
    for k, (dy, dc) in enumerate(RELATIVE):
        core = lax.rem(me, 2)
        core = 1 - core if dc else core
        h = lax.rem(lax.div(me, 2) + dy, SIDE) * 2 + core
        start = offset_ref[h]
        spots.append(start)
        mine = pltpu.roll(codes, lax.rem(ROWS_DEV - start, ROWS_DEV), 1)[:, :SLOTS]
        mine = jnp.where(slot < counts_ref[0, h], mine, -1).astype(F32)
        done_ref[k, SLOTS:LINES, 0:SLOTS] = split_rows(mine, SLOTS)
        done_ref[k, SLOTS:LINES, SLOTS:D] = jnp.zeros((EXTRA, D - SLOTS), BF)
    for c, p in zip(loads, parts):
        c.wait()
        for j in range(D // LANES):
            wide_ref[j, p, :] = vec_ref[p, j * LANES:(j + 1) * LANES].astype(F32)
    stores = [pltpu.make_async_copy(done_ref.at[k], outs[k], out_sems.at[k]) for k in range(GROUPS)]
    for k, start in enumerate(spots):
        for j in range(D // LANES):
            done_ref[k, 0:SLOTS, j * LANES:(j + 1) * LANES] = wide_ref[j, pl.ds(start, SLOTS), :].astype(BF)
        stores[k].start()
    for c in stores:
        c.wait()


def pack(counts, vectors, parents, children):
    return pl.pallas_call(
        pack_kernel,
        out_shape=[block_shape()] * GROUPS,
        in_specs=[pl.BlockSpec(memory_space=pltpu.HBM)] * 4,
        out_specs=[pl.BlockSpec(memory_space=pltpu.HBM)] * GROUPS,
        scratch_shapes=[
            pltpu.SMEM((1, GROUPS), I32),
            pltpu.VMEM((ROWS_DEV, D), BF),
            pltpu.VMEM((2, 1, ROWS_DEV), I32),
            pltpu.VMEM((D // LANES, ROWS_DEV + SLOTS, LANES), F32),
            pltpu.VMEM((GROUPS, LINES, D), BF),
            pltpu.SMEM((GROUPS,), I32),
            pltpu.SemaphoreType.DMA((3 + ROWS_DEV // SLOTS,)),
            pltpu.SemaphoreType.DMA((GROUPS,)),
        ],
        cost_estimate=cost(1e6, 3 * GROUPS * LINES * D),
        compiler_params=vmem(58),
        name="pack",
    )(counts, vectors, parents, children)


def codes_row(block_ref):
    return joined_rows(block_ref[SLOTS:LINES, 0:SLOTS])


def sums_kernel(stage, *refs):
    first, last = stage == 0, stage == len(STAGES) - 1
    n = len(STAGES[stage])
    blocks, refs = refs[:n], refs[n:]
    if not first:
        (old_ref, old_tally_ref), refs = refs[:2], refs[2:]
    place = lax.axis_index("mem")
    z, x = lax.div(place, SIDE), lax.rem(place, SIDE)
    codes = [codes_row(block).astype(I32) for block in blocks]
    line = lax.broadcasted_iota(I32, (TILE, SLOTS), 0)
    for t in range(2 * SIDE):
        k = t % SIDE
        base = lax.rem(x + k, SIDE) * TILE if t < SIDE else lax.rem(z + k, SIDE) * TILE + CHILD
        total = None
        tally = None
        for j in range(n):
            hit = jnp.where(line == codes[j] - base, 1.0, 0.0)
            count = hit[:, 0:LANES] + hit[:, LANES:SLOTS]
            part = jnp.dot(hit.astype(BF), blocks[j][0:SLOTS, :], preferred_element_type=F32)
            total = part if total is None else total + part
            tally = count if tally is None else tally + count
        if not first:
            total = total + old_ref[t]
            tally = tally + old_tally_ref[t]
        if last:
            out = refs[t]
            out[0:TILE, :] = total.astype(BF)
            out[TILE:LINES, 0:TILE] = split_rows(jnp.sum(tally.T, axis=0, keepdims=True), TILE)
            out[TILE:LINES, TILE:D] = jnp.zeros((EXTRA, D - TILE), BF)
        else:
            refs[0][t] = total
            refs[1][t] = tally


def sums(stage, blocks, old):
    first, last = stage == 0, stage == len(STAGES) - 1
    n = len(blocks)
    args = list(blocks) + ([] if first else list(old))
    tiles = [
        jax.ShapeDtypeStruct((2 * SIDE, TILE, D), F32),
        jax.ShapeDtypeStruct((2 * SIDE, TILE, LANES), F32),
    ]
    out_shape = [block_shape()] * (2 * SIDE) if last else tiles
    return pl.pallas_call(
        functools.partial(sums_kernel, stage),
        out_shape=out_shape,
        in_specs=[WHOLE] * len(args),
        out_specs=[WHOLE] * len(out_shape),
        input_output_aliases={} if first or last else {n: 0, n + 1: 1},
        cost_estimate=cost(4 * CHILD * n * SLOTS * D, 12 * CHILD * D),
        compiler_params=vmem(8),
        name="sums",
    )(*args)


def facts_kernel(*refs):
    blocks, (rows_ref, norm_ref, code_ref) = refs[:GROUPS], refs[GROUPS:]
    me = lax.axis_index("grp")
    for block, (dy, dc) in zip(blocks, RELATIVE):
        core = lax.rem(me, 2)
        core = 1 - core if dc else core
        source = lax.rem(lax.div(me, 2) + SIDE - dy, SIDE) * 2 + core
        at = pl.ds(pl.multiple_of(source * SLOTS, SLOTS), SLOTS)
        rows = block[0:SLOTS, :]
        rows_ref[at, :] = rows
        wide = rows.astype(F32)
        norm = jnp.sum(wide * wide, axis=1, keepdims=True) * (1.0 / D)
        norm_ref[at, :] = jnp.broadcast_to(norm, (SLOTS, LANES))
        code = jnp.broadcast_to(codes_row(block), (LANES, SLOTS)).T
        code_ref[at, :] = jnp.broadcast_to(code[:, 0:1], (SLOTS, LANES))


def facts(blocks):
    wide = jax.ShapeDtypeStruct((GROUPS * SLOTS, LANES), F32)
    return pl.pallas_call(
        facts_kernel,
        out_shape=[jax.ShapeDtypeStruct((GROUPS * SLOTS, D), BF), wide, wide],
        in_specs=[WHOLE] * GROUPS,
        out_specs=[WHOLE] * 3,
        cost_estimate=cost(1e6, 6 * GROUPS * SLOTS * D),
        compiler_params=vmem(8),
        name="facts",
    )(*blocks)


def total_of(parts):
    total = parts[0][0:TILE, :].astype(F32)
    tally = joined_rows(parts[0][TILE:LINES, 0:TILE])
    for part in parts[1:]:
        total = total + part[0:TILE, :].astype(F32)
        tally = tally + joined_rows(part[TILE:LINES, 0:TILE])
    return total, tally


def partial_kernel(a_ref, b_ref, c_ref, d_ref, out_ref):
    total, tally = total_of((a_ref, b_ref, c_ref, d_ref))
    out_ref[0:TILE, :] = total.astype(BF)
    out_ref[TILE:LINES, 0:TILE] = split_rows(tally, TILE)
    out_ref[TILE:LINES, TILE:D] = jnp.zeros((EXTRA, D - TILE), BF)


def mean_kernel(a_ref, b_ref, c_ref, d_ref, out_ref):
    total, tally = total_of((a_ref, b_ref, c_ref, d_ref))
    count = jnp.maximum(jnp.broadcast_to(tally, (LANES, TILE)).T[:, 0:1], 1.0)
    out_ref[...] = (total / count).astype(BF)


def reduce_four(kernel, name, lines, parts):
    return pl.pallas_call(
        kernel,
        out_shape=jax.ShapeDtypeStruct((lines, D), BF),
        in_specs=[WHOLE] * SIDE,
        out_specs=WHOLE,
        cost_estimate=cost(4 * TILE * D, 10 * TILE * D),
        compiler_params=vmem(8),
        name=name,
    )(*parts)


def square_row(cent_ref):
    wide = cent_ref[...].astype(F32)
    wide = wide * wide
    fold = wide[:, 0:LANES]
    for k in range(1, D // LANES):
        fold = fold + wide[:, k * LANES:(k + 1) * LANES]
    return jnp.sum(fold.T, axis=0, keepdims=True) * (1.0 / D)


def columns(spot, k):
    return pl.ds(pl.multiple_of(lax.rem(spot + SIDE - k, SIDE) * TILE, TILE), TILE)


def pieces(step, read, write, facts_at, low_ref, high_ref):
    place = lax.axis_index("mem")
    z, x = lax.div(place, SIDE), lax.rem(place, SIDE)
    rows, norm, code = facts_at
    norm = jnp.concatenate([norm, norm], axis=1)
    code = jnp.concatenate([code, code], axis=1)
    lower = jnp.logical_and(code >= 0.0, code < float(CHILD))
    upper = code >= float(CHILD)
    for spot, cent_ref, mine in ((x, low_ref, lower), (z, high_ref, upper)):
        cross = lax.dot_general(rows, cent_ref[...], (((1,), (1,)), ((), ())), preferred_element_type=F32)
        value = norm + square_row(cent_ref) - cross * (2.0 / D)
        at = columns(spot, step)
        write(at, jnp.where(mine, value, read(at)))


CHUNK = 512


def near_kernel(step, rows_ref, norm_ref, code_ref, low_ref, high_ref, *rest):
    out_ref = rest[-1]
    for i in range(GROUPS * SLOTS // CHUNK):
        at = slice(i * CHUNK, (i + 1) * CHUNK)
        if step == 0:
            out_ref[at, :] = jnp.zeros((CHUNK, CHILD), F32)

        def read(cols):
            return out_ref[at, cols]

        def write(cols, value):
            out_ref[at, cols] = value

        pieces(step, read, write, (rows_ref[at, :], norm_ref[at, :], code_ref[at, :]), low_ref, high_ref)


def near(step, told, low, high, old):
    args = [*told, low, high] + ([] if old is None else [old])
    return pl.pallas_call(
        functools.partial(near_kernel, step),
        out_shape=jax.ShapeDtypeStruct((GROUPS * SLOTS, CHILD), F32),
        in_specs=[WHOLE] * len(args),
        out_specs=WHOLE,
        input_output_aliases={} if old is None else {5: 0},
        cost_estimate=cost(CHILD * GROUPS * SLOTS * D, 4 * GROUPS * SLOTS * CHILD),
        compiler_params=vmem(8),
        name="near",
    )(*args)


def far_kernel(step, rows_ref, norm_ref, code_ref, low_ref, high_ref, old_ref, out_ref):
    at = pl.ds(pl.multiple_of(pl.program_id(0) * CHUNK, CHUNK), CHUNK)
    out_ref[...] = old_ref[at, :]

    def read(cols):
        return out_ref[:, cols]

    def write(cols, value):
        out_ref[:, cols] = value

    pieces(step, read, write, (rows_ref[at, :], norm_ref[at, :], code_ref[at, :]), low_ref, high_ref)


def far(step, told, low, high, old):
    return pl.pallas_call(
        functools.partial(far_kernel, step),
        grid=(GROUPS * SLOTS // CHUNK,),
        out_shape=jax.ShapeDtypeStruct((GROUPS * SLOTS, CHILD), F32),
        in_specs=[WHOLE] * 6,
        out_specs=pl.BlockSpec((CHUNK, CHILD), lambda i: (i, 0)),
        cost_estimate=cost(CHILD * GROUPS * SLOTS * D, 8 * GROUPS * SLOTS * CHILD),
        compiler_params=vmem(12),
        name="far",
    )(*told, low, high, old)


def along_grp(dy, dc):
    return [(y * 2 + c, ((y + dy) % SIDE) * 2 + (c ^ dc)) for y in range(SIDE) for c in range(2)]


def along_x(k):
    return [(z * SIDE + x, z * SIDE + (x + k) % SIDE) for z in range(SIDE) for x in range(SIDE)]


def along_z(k):
    return [(z * SIDE + x, ((z + k) % SIDE) * SIDE + x) for z in range(SIDE) for x in range(SIDE)]


def both(low, high, first, second):
    got_low, got_high = {}, {}
    for k in STEPS:
        got_low[k] = lax.ppermute(low[k], "mem", first(k))
        got_high[k] = lax.ppermute(high[k], "mem", second(k))
    return got_low, got_high


def body(vectors, parents, children, counts):
    parents = parents.reshape(1, ROWS_DEV)
    children = children.reshape(1, ROWS_DEV)
    packed = pack(counts, vectors, parents, children)
    arrived = [
        block if step == (0, 0) else lax.ppermute(block, "grp", along_grp(*step))
        for block, step in zip(packed, RELATIVE)
    ]
    tiles = None
    for stage, here in enumerate(STAGES):
        tiles = sums(stage, [arrived[k] for k in here], tiles)
    low, high = tiles[:SIDE], tiles[SIDE:]
    told = facts(arrived)

    got_low, got_high = both(low, high, along_x, along_z)
    got_low, told = lax.optimization_barrier((got_low, told))
    low = reduce_four(partial_kernel, "partial", LINES, [low[0]] + [got_low[k] for k in STEPS])
    high = reduce_four(partial_kernel, "partial", LINES, [high[0]] + [got_high[k] for k in STEPS])

    got_low, got_high = both([low] * SIDE, [high] * SIDE, along_z, along_x)
    low = reduce_four(mean_kernel, "mean", TILE, [low] + [got_low[k] for k in STEPS])
    high = reduce_four(mean_kernel, "mean", TILE, [high] + [got_high[k] for k in STEPS])

    got_low, got_high = both([low] * SIDE, [high] * SIDE, along_x, along_z)
    out = near(0, told, low, high, None)
    for k in STEPS[:2]:
        out = near(k, told, got_low[k], got_high[k], out)
    return far(STEPS[2], told, got_low[STEPS[2]], got_high[STEPS[2]], out)


def solution(mesh):
    in_specs = (
        P(("grp", "mem"), None),
        P(("grp", "mem")),
        P(("grp", "mem")),
        P(("grp", "mem"), None),
    )
    out_specs = P(("grp", "mem"), None)
    return jax.shard_map(body, mesh=mesh, in_specs=in_specs, out_specs=out_specs, check_vma=False)
```

```python
import functools

import jax
import jax.numpy as jnp
from jax import lax
from jax.experimental import pallas as pl
from jax.experimental.pallas import tpu as pltpu
from jax.sharding import PartitionSpec as P

D = 768
CHILD = 1024
GROUPS = 8
SLOTS = 256
ROWS_DEV = 1024
LANES = 128
SIDE = 4
TILE = CHILD // SIDE
EXTRA = 8
LINES = TILE + EXTRA

BF = jnp.bfloat16
F32 = jnp.float32
I32 = jnp.int32
WHOLE = pl.BlockSpec(memory_space=pltpu.VMEM)

RELATIVE = ((0, 0), (0, 1), (1, 0), (1, 1), (3, 0), (3, 1), (2, 0), (2, 1))
WIDTHS = (512, 256)
STAGES = (((0, 1), (2, 4), (3, 5, 6, 7)), ((0, 1, 2, 4), (3, 5, 6, 7)))
STEPS = (1, 3, 2)


def cost(flops, nbytes):
    return pl.CostEstimate(flops=int(flops), bytes_accessed=int(nbytes), transcendentals=0)


def vmem(mib):
    return pltpu.CompilerParams(vmem_limit_bytes=mib << 20)


def block_shape(chunk):
    return jax.ShapeDtypeStruct((TILE if chunk else LINES, WIDTHS[chunk]), BF)


def split_rows(values, width):
    high = jnp.floor(values * (1.0 / 128.0))
    low = values - high * 128.0
    line = lax.broadcasted_iota(I32, (EXTRA, width), 0)
    return jnp.where(line == 0, high, jnp.where(line == 1, low, 0.0)).astype(BF)


def joined_rows(block):
    wide = block.astype(F32)
    return wide[0:1, :] * 128.0 + wide[1:2, :]


def pack_kernel(counts_hbm, vec_hbm, par_hbm, chi_hbm, *rest):
    outs, rest = rest[:2 * GROUPS], rest[2 * GROUPS:]
    counts_ref, vec_ref, ids_ref, wide_ref, done_ref, offset_ref, sems, out_sems = rest
    me = lax.axis_index("grp")
    small = [
        pltpu.make_async_copy(counts_hbm, counts_ref, sems.at[0]),
        pltpu.make_async_copy(par_hbm, ids_ref.at[0], sems.at[1]),
        pltpu.make_async_copy(chi_hbm, ids_ref.at[1], sems.at[2]),
    ]
    parts = [pl.ds(n * SLOTS, SLOTS) for n in range(ROWS_DEV // SLOTS)]
    loads = [pltpu.make_async_copy(vec_hbm.at[p], vec_ref.at[p], sems.at[3 + n]) for n, p in enumerate(parts)]
    for c in small + loads:
        c.start()
    for j in range(D // LANES):
        wide_ref[j, ROWS_DEV:ROWS_DEV + SLOTS, :] = jnp.zeros((SLOTS, LANES), F32)
    for c in small:
        c.wait()
    offset = 0
    for h in range(GROUPS):
        offset_ref[h] = offset
        offset = offset + counts_ref[0, h]
    codes = ids_ref[0] * CHILD + ids_ref[1]
    slot = lax.broadcasted_iota(I32, (1, SLOTS), 1)
    spots = []
    for k, (dy, dc) in enumerate(RELATIVE):
        core = lax.rem(me, 2)
        core = 1 - core if dc else core
        h = lax.rem(lax.div(me, 2) + dy, SIDE) * 2 + core
        start = offset_ref[h]
        spots.append(start)
        mine = pltpu.roll(codes, lax.rem(ROWS_DEV - start, ROWS_DEV), 1)[:, :SLOTS]
        mine = jnp.where(slot < counts_ref[0, h], mine, -1).astype(F32)
        done_ref[k, SLOTS:LINES, 0:SLOTS] = split_rows(mine, SLOTS)
        done_ref[k, SLOTS:LINES, SLOTS:D] = jnp.zeros((EXTRA, D - SLOTS), BF)
    for c, p in zip(loads, parts):
        c.wait()
        for j in range(D // LANES):
            wide_ref[j, p, :] = vec_ref[p, j * LANES:(j + 1) * LANES].astype(F32)
    stores = []
    for chunk, (at, lines) in enumerate(((slice(0, WIDTHS[0]), LINES), (slice(WIDTHS[0], D), SLOTS))):
        for k, start in enumerate(spots):
            for j in range(at.start // LANES, at.stop // LANES):
                done_ref[k, 0:SLOTS, j * LANES:(j + 1) * LANES] = wide_ref[j, pl.ds(start, SLOTS), :].astype(BF)
            n = chunk * GROUPS + k
            stores.append(pltpu.make_async_copy(done_ref.at[k, 0:lines, at], outs[n], out_sems.at[n]))
            stores[-1].start()
    for c in stores:
        c.wait()


def pack(counts, vectors, parents, children):
    return pl.pallas_call(
        pack_kernel,
        out_shape=[block_shape(0)] * GROUPS + [block_shape(1)] * GROUPS,
        in_specs=[pl.BlockSpec(memory_space=pltpu.HBM)] * 4,
        out_specs=[pl.BlockSpec(memory_space=pltpu.HBM)] * (2 * GROUPS),
        scratch_shapes=[
            pltpu.SMEM((1, GROUPS), I32),
            pltpu.VMEM((ROWS_DEV, D), BF),
            pltpu.VMEM((2, 1, ROWS_DEV), I32),
            pltpu.VMEM((D // LANES, ROWS_DEV + SLOTS, LANES), F32),
            pltpu.VMEM((GROUPS, LINES, D), BF),
            pltpu.SMEM((GROUPS,), I32),
            pltpu.SemaphoreType.DMA((3 + ROWS_DEV // SLOTS,)),
            pltpu.SemaphoreType.DMA((2 * GROUPS,)),
        ],
        cost_estimate=cost(1e6, 3 * GROUPS * LINES * D),
        compiler_params=vmem(58),
        name="pack",
    )(counts, vectors, parents, children)


def codes_row(block_ref):
    return joined_rows(block_ref[SLOTS:LINES, 0:SLOTS])


def sums_kernel(chunk, stage, *refs):
    stages = STAGES[chunk]
    first, last, width = stage == 0, stage == len(stages) - 1, WIDTHS[chunk]
    n = len(stages[stage])
    carriers, refs = refs[:n], refs[n:]
    blocks = carriers
    if chunk:
        blocks, refs = refs[:n], refs[n:]
    old_ref = old_tally_ref = None
    if not first:
        old_ref, refs = refs[0], refs[1:]
        if not chunk:
            old_tally_ref, refs = refs[0], refs[1:]
    place = lax.axis_index("mem")
    z, x = lax.div(place, SIDE), lax.rem(place, SIDE)
    codes = [codes_row(block).astype(I32) for block in carriers]
    line = lax.broadcasted_iota(I32, (TILE, SLOTS), 0)
    for t in range(2 * SIDE):
        k = t % SIDE
        base = lax.rem(x + k, SIDE) * TILE if t < SIDE else lax.rem(z + k, SIDE) * TILE + CHILD
        total = None
        tally = None
        for j in range(n):
            hit = jnp.where(line == codes[j] - base, 1.0, 0.0)
            part = jnp.dot(hit.astype(BF), blocks[j][0:SLOTS, :], preferred_element_type=F32)
            total = part if total is None else total + part
            if not chunk:
                count = hit[:, 0:LANES] + hit[:, LANES:SLOTS]
                tally = count if tally is None else tally + count
        if not first:
            total = total + old_ref[t]
            if not chunk:
                tally = tally + old_tally_ref[t]
        if last:
            out = refs[t]
            out[0:TILE, :] = total.astype(BF)
            if not chunk:
                out[TILE:LINES, 0:TILE] = split_rows(jnp.sum(tally.T, axis=0, keepdims=True), TILE)
                out[TILE:LINES, TILE:width] = jnp.zeros((EXTRA, width - TILE), BF)
        else:
            refs[0][t] = total
            if not chunk:
                refs[1][t] = tally


def sums(chunk, stage, carriers, blocks, old):
    first, last = stage == 0, stage == len(STAGES[chunk]) - 1
    given = list(carriers) + (list(blocks) if chunk else [])
    args = given + ([] if first else list(old))
    out_shape = [jax.ShapeDtypeStruct((2 * SIDE, TILE, WIDTHS[chunk]), F32)]
    if not chunk:
        out_shape.append(jax.ShapeDtypeStruct((2 * SIDE, TILE, LANES), F32))
    aliases = {} if first or last else {len(given) + i: i for i in range(len(out_shape))}
    if last:
        out_shape = [block_shape(chunk)] * (2 * SIDE)
    return pl.pallas_call(
        functools.partial(sums_kernel, chunk, stage),
        out_shape=out_shape,
        in_specs=[WHOLE] * len(args),
        out_specs=[WHOLE] * len(out_shape),
        input_output_aliases=aliases,
        cost_estimate=cost(4 * CHILD * len(carriers) * SLOTS * WIDTHS[chunk], 12 * CHILD * WIDTHS[chunk]),
        compiler_params=vmem(8),
        name="sums",
    )(*args)


def facts_kernel(*refs):
    blocks, tails = refs[:GROUPS], refs[GROUPS:2 * GROUPS]
    rows_ref, norm_ref, code_ref = refs[2 * GROUPS:]
    me = lax.axis_index("grp")
    for block, tail, (dy, dc) in zip(blocks, tails, RELATIVE):
        core = lax.rem(me, 2)
        core = 1 - core if dc else core
        source = lax.rem(lax.div(me, 2) + SIDE - dy, SIDE) * 2 + core
        at = pl.ds(pl.multiple_of(source * SLOTS, SLOTS), SLOTS)
        rows = jnp.concatenate([block[0:SLOTS, :], tail[...]], axis=1)
        rows_ref[at, :] = rows
        wide = rows.astype(F32)
        norm = jnp.sum(wide * wide, axis=1, keepdims=True) * (1.0 / D)
        norm_ref[at, :] = jnp.broadcast_to(norm, (SLOTS, LANES))
        code = jnp.broadcast_to(codes_row(block), (LANES, SLOTS)).T
        code_ref[at, :] = jnp.broadcast_to(code[:, 0:1], (SLOTS, LANES))


def facts(blocks):
    wide = jax.ShapeDtypeStruct((GROUPS * SLOTS, LANES), F32)
    return pl.pallas_call(
        facts_kernel,
        out_shape=[jax.ShapeDtypeStruct((GROUPS * SLOTS, D), BF), wide, wide],
        in_specs=[WHOLE] * (2 * GROUPS),
        out_specs=[WHOLE] * 3,
        cost_estimate=cost(1e6, 6 * GROUPS * SLOTS * D),
        compiler_params=vmem(8),
        name="facts",
    )(*blocks)


def total_of(parts):
    total = parts[0][0:TILE, :].astype(F32)
    tally = joined_rows(parts[0][TILE:LINES, 0:TILE])
    for part in parts[1:]:
        total = total + part[0:TILE, :].astype(F32)
        tally = tally + joined_rows(part[TILE:LINES, 0:TILE])
    return total, tally


def partial_kernel(*refs):
    parts, tails, out_ref = refs[:SIDE], refs[SIDE:2 * SIDE], refs[2 * SIDE]
    total, tally = total_of(parts)
    tail = tails[0][...].astype(F32)
    for part in tails[1:]:
        tail = tail + part[...].astype(F32)
    out_ref[0:TILE, 0:WIDTHS[0]] = total.astype(BF)
    out_ref[0:TILE, WIDTHS[0]:D] = tail.astype(BF)
    out_ref[TILE:LINES, 0:TILE] = split_rows(tally, TILE)
    out_ref[TILE:LINES, TILE:D] = jnp.zeros((EXTRA, D - TILE), BF)


def mean_kernel(a_ref, b_ref, c_ref, d_ref, out_ref):
    total, tally = total_of((a_ref, b_ref, c_ref, d_ref))
    count = jnp.maximum(jnp.broadcast_to(tally, (LANES, TILE)).T[:, 0:1], 1.0)
    out_ref[...] = (total / count).astype(BF)


def reduce_four(kernel, name, lines, parts):
    return pl.pallas_call(
        kernel,
        out_shape=jax.ShapeDtypeStruct((lines, D), BF),
        in_specs=[WHOLE] * len(parts),
        out_specs=WHOLE,
        cost_estimate=cost(4 * TILE * D, 10 * TILE * D),
        compiler_params=vmem(8),
        name=name,
    )(*parts)


def square_row(cent_ref):
    wide = cent_ref[...].astype(F32)
    wide = wide * wide
    fold = wide[:, 0:LANES]
    for k in range(1, D // LANES):
        fold = fold + wide[:, k * LANES:(k + 1) * LANES]
    return jnp.sum(fold.T, axis=0, keepdims=True) * (1.0 / D)


def columns(spot, k):
    return pl.ds(pl.multiple_of(lax.rem(spot + SIDE - k, SIDE) * TILE, TILE), TILE)


def pieces(step, read, write, facts_at, low_ref, high_ref):
    place = lax.axis_index("mem")
    z, x = lax.div(place, SIDE), lax.rem(place, SIDE)
    rows, norm, code = facts_at
    norm = jnp.concatenate([norm, norm], axis=1)
    code = jnp.concatenate([code, code], axis=1)
    lower = jnp.logical_and(code >= 0.0, code < float(CHILD))
    upper = code >= float(CHILD)
    for spot, cent_ref, mine in ((x, low_ref, lower), (z, high_ref, upper)):
        cross = lax.dot_general(rows, cent_ref[...], (((1,), (1,)), ((), ())), preferred_element_type=F32)
        value = norm + square_row(cent_ref) - cross * (2.0 / D)
        at = columns(spot, step)
        write(at, jnp.where(mine, value, read(at)))


CHUNK = 512


def near_kernel(step, rows_ref, norm_ref, code_ref, low_ref, high_ref, *rest):
    out_ref = rest[-1]
    for i in range(GROUPS * SLOTS // CHUNK):
        at = slice(i * CHUNK, (i + 1) * CHUNK)
        if step == 0:
            out_ref[at, :] = jnp.zeros((CHUNK, CHILD), F32)

        def read(cols):
            return out_ref[at, cols]

        def write(cols, value):
            out_ref[at, cols] = value

        pieces(step, read, write, (rows_ref[at, :], norm_ref[at, :], code_ref[at, :]), low_ref, high_ref)


def near(step, told, low, high, old):
    args = [*told, low, high] + ([] if old is None else [old])
    return pl.pallas_call(
        functools.partial(near_kernel, step),
        out_shape=jax.ShapeDtypeStruct((GROUPS * SLOTS, CHILD), F32),
        in_specs=[WHOLE] * len(args),
        out_specs=WHOLE,
        input_output_aliases={} if old is None else {5: 0},
        cost_estimate=cost(CHILD * GROUPS * SLOTS * D, 4 * GROUPS * SLOTS * CHILD),
        compiler_params=vmem(8),
        name="near",
    )(*args)


def far_kernel(step, rows_ref, norm_ref, code_ref, low_ref, high_ref, old_ref, out_ref):
    at = pl.ds(pl.multiple_of(pl.program_id(0) * CHUNK, CHUNK), CHUNK)
    out_ref[...] = old_ref[at, :]

    def read(cols):
        return out_ref[:, cols]

    def write(cols, value):
        out_ref[:, cols] = value

    pieces(step, read, write, (rows_ref[at, :], norm_ref[at, :], code_ref[at, :]), low_ref, high_ref)


def far(step, told, low, high, old):
    return pl.pallas_call(
        functools.partial(far_kernel, step),
        grid=(GROUPS * SLOTS // CHUNK,),
        out_shape=jax.ShapeDtypeStruct((GROUPS * SLOTS, CHILD), F32),
        in_specs=[WHOLE] * 6,
        out_specs=pl.BlockSpec((CHUNK, CHILD), lambda i: (i, 0)),
        cost_estimate=cost(CHILD * GROUPS * SLOTS * D, 8 * GROUPS * SLOTS * CHILD),
        compiler_params=vmem(12),
        name="far",
    )(*told, low, high, old)


def along_grp(dy, dc):
    return [(y * 2 + c, ((y + dy) % SIDE) * 2 + (c ^ dc)) for y in range(SIDE) for c in range(2)]


def along_x(k):
    return [(z * SIDE + x, z * SIDE + (x + k) % SIDE) for z in range(SIDE) for x in range(SIDE)]


def along_z(k):
    return [(z * SIDE + x, ((z + k) % SIDE) * SIDE + x) for z in range(SIDE) for x in range(SIDE)]


def both(low, high, first, second):
    got_low, got_high = {}, {}
    for k in STEPS:
        got_low[k] = lax.ppermute(low[k], "mem", first(k))
        got_high[k] = lax.ppermute(high[k], "mem", second(k))
    return got_low, got_high


def body(vectors, parents, children, counts):
    parents = parents.reshape(1, ROWS_DEV)
    children = children.reshape(1, ROWS_DEV)
    packed = pack(counts, vectors, parents, children)
    arrived = [
        [
            block if step == (0, 0) else lax.ppermute(block, "grp", along_grp(*step))
            for block, step in zip(packed[chunk * GROUPS:(chunk + 1) * GROUPS], RELATIVE)
        ]
        for chunk in range(2)
    ]
    lows, highs = [], []
    for chunk in range(2):
        tiles = None
        for stage, here in enumerate(STAGES[chunk]):
            tiles = sums(chunk, stage, [arrived[0][k] for k in here], [arrived[chunk][k] for k in here], tiles)
        low, high = tiles[:SIDE], tiles[SIDE:]
        got_low, got_high = both(low, high, along_x, along_z)
        lows += [low[0]] + [got_low[k] for k in STEPS]
        highs += [high[0]] + [got_high[k] for k in STEPS]
    told = facts(arrived[0] + arrived[1])
    lows, told = lax.optimization_barrier((lows, told))
    low = reduce_four(partial_kernel, "partial", LINES, lows)
    high = reduce_four(partial_kernel, "partial", LINES, highs)

    got_low, got_high = both([low] * SIDE, [high] * SIDE, along_z, along_x)
    low = reduce_four(mean_kernel, "mean", TILE, [low] + [got_low[k] for k in STEPS])
    high = reduce_four(mean_kernel, "mean", TILE, [high] + [got_high[k] for k in STEPS])

    got_low, got_high = both([low] * SIDE, [high] * SIDE, along_x, along_z)
    out = near(0, told, low, high, None)
    for k in STEPS[:2]:
        out = near(k, told, got_low[k], got_high[k], out)
    return far(STEPS[2], told, got_low[STEPS[2]], got_high[STEPS[2]], out)


def solution(mesh):
    in_specs = (
        P(("grp", "mem"), None),
        P(("grp", "mem")),
        P(("grp", "mem")),
        P(("grp", "mem"), None),
    )
    out_specs = P(("grp", "mem"), None)
    return jax.shard_map(body, mesh=mesh, in_specs=in_specs, out_specs=out_specs, check_vma=False)
```
